32 devices in a mesh: ctx: 8 (over z, y), fsdp: 4 (over x, core).
Axes of the slice: x: 2, y: 2, z: 4, core: 2. Of those that a mesh axis runs over, the one named last changes fastest.
Arguments:
- query_rows: bfloat16 [8192, 4096], P('ctx', 'fsdp'), may hold values from -6 to 6
- key_rows: bfloat16 [8192, 4096], P('ctx', 'fsdp'), may hold values from -6 to 6
- value_rows: bfloat16 [8192, 4096], P('ctx', 'fsdp'), may hold values from -25 to 25
- norm_gain: bfloat16 [4096], P('fsdp'), may hold values from 0.099609375 to 1.8984375
- out_grad: bfloat16 [8192, 4096], P('ctx', 'fsdp'), may hold values from -6 to 6
Outputs:
- attended: bfloat16 [8192, 4096], P('ctx', 'fsdp')
- query_grad: bfloat16 [8192, 4096], P('ctx', 'fsdp')
- key_grad: bfloat16 [8192, 4096], P('ctx', 'fsdp')
- value_grad: bfloat16 [8192, 4096], P('ctx', 'fsdp')
The draws below stay inside these ranges and needn't reach their ends.
All inputs are finite; a program needn't handle non-finite values.
Results may differ from the reference program's by a relative error of at most 0.0058.
Values sent between devices are 32-bit elements; how exact they have to be, the bound alone decides.
No kernel may reach another device: no remote copies, remote signals or barrier semaphores. Data moves between devices by JAX's collectives and lax.ppermute only.
A program may use at most 128 MiB of HBM per device.

```python
import jax
import jax.numpy as jnp
from jax import lax

HEADS = 32
HEAD_DIM = 128
TOK_DEV = 1024
TOKENS = 8192
N_CTX = 8


def draw_value_rows(key, part):
    width = HEADS * HEAD_DIM
    key_base = jax.random.fold_in(key, 11)
    key_jitter = jax.random.fold_in(key, 12)
    position = jnp.arange(width, dtype=jnp.float32) / (width - 1)
    jitter = jax.random.uniform(key_jitter, (width,), jnp.float32, 0.7, 1.3)
    column_scale = jnp.exp(jnp.log(10.0) * (position - 0.5)) * jitter
    base = jnp.clip(jax.random.normal(key_base, (TOKENS, width), jnp.float32), -6.0, 6.0)
    values = base * column_scale
    return values.astype(jnp.bfloat16)


def levels(stream_key, extent, cuts, low, largest):
    level, own = 1.0, jax.random.fold_in(stream_key, 6)
    for dim, parts in cuts:
        draws = jnp.exp(jax.random.uniform(jax.random.fold_in(own, dim), (parts,), jnp.float32, low / len(cuts), largest / len(cuts)))
        level = level * jnp.repeat(draws, extent[dim] // parts).reshape([-1 if axis == dim else 1 for axis in range(len(extent))])
    return level


def gaussian(key, shape, scale, reach, pieces=(), held_as=jnp.bfloat16):
    loudness = levels(key, shape, pieces, -0.22, 0.18) if pieces else 1.0
    values = jax.random.normal(key, shape, jnp.float32) * scale * loudness
    return jnp.minimum(jnp.maximum(values, -reach), reach).astype(held_as)


def setup_inputs(seed: int = 0) -> dict:
    key_of = jax.random.split(jax.random.key(seed), 6)
    return {
        "query_rows": gaussian(key_of[0], (TOKENS, HEADS * HEAD_DIM), 1.0, 6.0, ((0, 8), (1, 4))),
        "key_rows": gaussian(key_of[1], (TOKENS, HEADS * HEAD_DIM), 1.0, 6.0, ((0, 8), (1, 4))),
        "value_rows": draw_value_rows(jax.random.fold_in(key_of[5], 71), 0),
        "norm_gain": jnp.clip(1.0 + 0.18 * jax.random.normal(key_of[3], (HEADS * HEAD_DIM,), jnp.float32), 0.099609375, 1.8984375).astype(jnp.bfloat16),
        "out_grad": gaussian(key_of[4], (TOKENS, HEADS * HEAD_DIM), 1.0, 6.0, ((0, 8), (1, 4))),
    }


def to_half(x):
    return lax.optimization_barrier(x.astype(jnp.bfloat16)).astype(jnp.float32)

def reference(query_rows, key_rows, value_rows, norm_gain, out_grad):
    shape4 = (N_CTX, TOK_DEV, HEADS, HEAD_DIM)
    width = HEADS * HEAD_DIM
    queries = query_rows.reshape(shape4).astype(jnp.float32)
    keys_all = key_rows.reshape(shape4).astype(jnp.float32)
    values_all = value_rows.reshape(shape4).astype(jnp.float32)
    cotangent = out_grad.reshape(N_CTX, TOK_DEV, width).astype(jnp.float32)
    gain = norm_gain.astype(jnp.float32)
    causal = jnp.arange(TOK_DEV)[:, None] >= jnp.arange(TOK_DEV)[None, :]

    def local_state(pair):
        return jnp.einsum('shd,she->hde', pair[0], pair[1])
    states = lax.map(local_state, (keys_all, values_all))
    zero = jnp.zeros((1, HEADS, HEAD_DIM, HEAD_DIM), jnp.float32)
    prefix = to_half(jnp.concatenate([zero, jnp.cumsum(states, 0)[:-1]], 0))

    def forward_block(items):
        qb, kb, vb, pb, dyb = items
        scores = jnp.einsum('thd,shd->hts', qb, kb)
        probs = to_half(jnp.where(causal[None], scores, 0.0))
        mixed = jnp.einsum('hts,she->the', probs, vb) + jnp.einsum('thd,hde->the', qb, pb)
        mixed = mixed.reshape(TOK_DEV, width)
        inverse = lax.rsqrt(lax.optimization_barrier(jnp.sum(mixed * mixed, 1)) / width + 1e-06)
        attended = (mixed * inverse[:, None] * gain).astype(jnp.bfloat16)
        weighted = dyb * gain
        cross = lax.optimization_barrier(jnp.sum(weighted * mixed, 1))
        factor = inverse * inverse * cross / width
        mixed_grad = to_half(inverse[:, None] * (weighted - mixed * factor[:, None]))
        mixed_grad = mixed_grad.reshape(TOK_DEV, HEADS, HEAD_DIM)
        grad_state = jnp.einsum('thd,the->hde', qb, mixed_grad)
        return (attended, mixed_grad, grad_state)
    attended, mixed_grads, grad_states = lax.map(forward_block, (queries, keys_all, values_all, prefix, cotangent))
    reverse_sum = jnp.cumsum(grad_states[::-1], 0)[::-1]
    suffix = to_half(jnp.concatenate([reverse_sum[1:], zero], 0))

    def backward_block(items):
        qb, kb, vb, pb, sb, mg = items
        scores = jnp.einsum('thd,shd->hts', qb, kb)
        probs = to_half(jnp.where(causal[None], scores, 0.0))
        score_grad = to_half(jnp.where(causal[None], jnp.einsum('the,she->hts', mg, vb), 0.0))
        dquery = jnp.einsum('hts,shd->thd', score_grad, kb) + jnp.einsum('the,hde->thd', mg, pb)
        dkey = jnp.einsum('hts,thd->shd', score_grad, qb) + jnp.einsum('she,hde->shd', vb, sb)
        dvalue = jnp.einsum('hts,the->she', probs, mg) + jnp.einsum('shd,hde->she', kb, sb)
        return (dquery.astype(jnp.bfloat16), dkey.astype(jnp.bfloat16), dvalue.astype(jnp.bfloat16))
    dquery, dkey, dvalue = lax.map(backward_block, (queries, keys_all, values_all, prefix, suffix, mixed_grads))
    flat = (TOKENS, width)
    return (attended.reshape(flat), dquery.reshape(flat), dkey.reshape(flat), dvalue.reshape(flat))
```

```python
import functools

import jax
import jax.numpy as jnp
from jax import lax
from jax.experimental import pallas as pl
from jax.experimental.pallas import tpu as pltpu
from jax.sharding import PartitionSpec as P

HEADS = 32
HEAD_DIM = 128
GROUP = 4
CHUNK = 256

F32 = jnp.float32
BF16 = jnp.bfloat16
D = HEAD_DIM


def nn(a, b):
    return lax.dot_general(a, b, (((1,), (0,)), ((), ())), preferred_element_type=F32)


def nt(a, b):
    return lax.dot_general(a, b, (((1,), (1,)), ((), ())), preferred_element_type=F32)


def tn(a, b):
    return lax.dot_general(a, b, (((0,), (0,)), ((), ())), preferred_element_type=F32)


def head_cols(quarter, j, per):
    return pl.ds(pl.multiple_of((quarter * per + j) * D, D), D)


def call(kernel, name, outs, args, flops, scratch=(), hbm_outs=0, vmem=8):
    def spec(x):
        if x.dtype == jnp.int32:
            return pl.BlockSpec(memory_space=pltpu.SMEM)
        return pl.BlockSpec(memory_space=pltpu.VMEM)

    size = sum(x.size * x.dtype.itemsize for x in args)
    return pl.pallas_call(
        kernel,
        name=name,
        out_shape=outs,
        in_specs=[spec(x) for x in args],
        out_specs=[pl.BlockSpec(memory_space=pltpu.VMEM) for _ in outs],
        scratch_shapes=list(scratch),
        cost_estimate=pl.CostEstimate(flops=flops, bytes_accessed=size, transcendentals=0),
        compiler_params=pltpu.CompilerParams(vmem_limit_bytes=vmem << 20),
    )(*args)


def state_kernel(slots, per, me_ref, a_ref, b_ref, *out_refs):
    me = me_ref[0]
    for s, out_ref in zip(slots, out_refs):
        for j in range(per):
            cols = head_cols(me ^ s, j, per)
            out_ref[pl.ds(j * D, D), :] = tn(a_ref[:, cols], b_ref[:, cols])


def intra_kernel(q_ref, k_ref, v_ref, mixed_ref, qt_ref):
    tokens, width = q_ref.shape
    row = lax.broadcasted_iota(jnp.int32, (CHUNK, CHUNK), 0)
    col = lax.broadcasted_iota(jnp.int32, (CHUNK, CHUNK), 1)
    causal = row >= col

    @pl.loop(0, width // D)
    def _(h):
        cols = pl.ds(pl.multiple_of(h * D, D), D)
        state = jnp.zeros((D, D), F32)
        for c in range(tokens // CHUNK):
            rows = pl.ds(c * CHUNK, CHUNK)
            q, k, v = q_ref[rows, cols], k_ref[rows, cols], v_ref[rows, cols]
            probs = jnp.where(causal, nt(q, k), 0.0).astype(BF16)
            out = nn(probs, v)
            if c > 0:
                out = out + nn(q, state.astype(BF16))
            mixed_ref[rows, cols] = out
            if (c + 1) * CHUNK < tokens:
                state = state + tn(k, v)
            qt_ref[cols, rows] = q.T


def mix_kernel(per, me_ref, q_ref, intra_ref, dy_ref, gain_ref, e0, e1, e2, e3, mixed_ref, red_ref, sq, cr):
    tokens = q_ref.shape[0]
    me = me_ref[0]
    first = True
    for s, e_ref in enumerate((e0, e1, e2, e3)):
        for j in range(per):
            cols = head_cols(me ^ s, j, per)
            prefix = e_ref[pl.ds(j * D, D), :].astype(BF16)
            gain = gain_ref[:, cols].astype(F32)
            for c in range(tokens // CHUNK):
                rows = pl.ds(c * CHUNK, CHUNK)
                mixed = intra_ref[rows, cols] + nn(q_ref[rows, cols], prefix)
                mixed_ref[rows, cols] = mixed
                weighted = dy_ref[rows, cols].astype(F32) * gain
                if first:
                    sq[rows, :] = mixed * mixed
                    cr[rows, :] = weighted * mixed
                else:
                    sq[rows, :] += mixed * mixed
                    cr[rows, :] += weighted * mixed
            first = False
    ones = jnp.ones((8, D), F32)
    dims = (((1,), (1,)), ((), ()))
    for i, acc in enumerate((sq, cr)):
        total = lax.dot_general(ones, acc[...], dims, precision=lax.Precision.HIGHEST, preferred_element_type=F32)
        red_ref[pl.ds(i, 1), :] = total[:1]


def row_scales(red_ref, full_width):
    inverse = lax.rsqrt(red_ref[0:1, :] / full_width + 1e-06)
    factor = inverse * inverse * red_ref[1:2, :] / full_width
    return inverse, factor


def spread(row):
    return jnp.broadcast_to(row, (D, row.shape[1])).T


def grad_kernel(slots, per, full_width, me_ref, qt_ref, mixed_ref, dy_ref, gain_ref, red_ref, mg_ref, *out_refs):
    tokens = mixed_ref.shape[0]
    me = me_ref[0]
    inverse, factor = row_scales(red_ref, full_width)
    inverse, factor = spread(inverse), spread(factor)
    for s, out_ref in zip(slots, out_refs):
        for j in range(per):
            cols = head_cols(me ^ s, j, per)
            gain = gain_ref[:, cols].astype(F32)
            state = jnp.zeros((D, D), F32)
            for c in range(tokens // CHUNK):
                rows = pl.ds(c * CHUNK, CHUNK)
                part = slice(c * CHUNK, (c + 1) * CHUNK)
                weighted = dy_ref[rows, cols].astype(F32) * gain
                mg = (inverse[part] * (weighted - mixed_ref[rows, cols] * factor[part])).astype(BF16)
                mg_ref[rows, cols] = mg
                state = state + nn(qt_ref[cols, rows], mg)
            out_ref[pl.ds(j * D, D), :] = state


def query_kernel(per, full_width, me_ref, k_ref, v_ref, mg_ref, mixed_ref, gain_ref, red_ref, e0, e1, e2, e3, att_ref, dq_ref):
    tokens, width = k_ref.shape
    me = me_ref[0]
    row = lax.broadcasted_iota(jnp.int32, (CHUNK, CHUNK), 0)
    col = lax.broadcasted_iota(jnp.int32, (CHUNK, CHUNK), 1)
    causal = row >= col
    inverse, _ = row_scales(red_ref, full_width)
    inverse = spread(inverse)
    for s, e_ref in enumerate((e0, e1, e2, e3)):
        for j in range(per):
            cols = head_cols(me ^ s, j, per)
            gain = gain_ref[:, cols].astype(F32)
            state = e_ref[pl.ds(j * D, D), :]
            for c in range(tokens // CHUNK):
                rows = pl.ds(c * CHUNK, CHUNK)
                part = slice(c * CHUNK, (c + 1) * CHUNK)
                k, v, mg = k_ref[rows, cols], v_ref[rows, cols], mg_ref[rows, cols]
                ds = jnp.where(causal, nt(mg, v), 0.0).astype(BF16)
                dq_ref[rows, cols] = (nn(ds, k) + nt(mg, state.astype(BF16))).astype(BF16)
                att_ref[rows, cols] = (mixed_ref[rows, cols] * inverse[part] * gain).astype(BF16)
                if (c + 1) * CHUNK < tokens:
                    state = state + tn(k, v)


def keyvalue_kernel(q_ref, k_ref, v_ref, qt_ref, mg_ref, dk_ref, dv_ref):
    tokens, width = q_ref.shape
    row = lax.broadcasted_iota(jnp.int32, (CHUNK, CHUNK), 0)
    col = lax.broadcasted_iota(jnp.int32, (CHUNK, CHUNK), 1)
    causal = row <= col

    @pl.loop(0, width // D)
    def _(h):
        cols = pl.ds(pl.multiple_of(h * D, D), D)
        state = jnp.zeros((D, D), F32)
        for c in reversed(range(tokens // CHUNK)):
            rows = pl.ds(c * CHUNK, CHUNK)
            q, k, v, mg = q_ref[rows, cols], k_ref[rows, cols], v_ref[rows, cols], mg_ref[rows, cols]
            probs = jnp.where(causal, nt(k, q), 0.0).astype(BF16)
            ds = jnp.where(causal, nt(v, mg), 0.0).astype(BF16)
            dk, dv = nn(ds, q), nn(probs, mg)
            if (c + 1) * CHUNK < tokens:
                later = state.astype(BF16)
                dk = dk + nt(v, later)
                dv = dv + nn(k, later)
            dk_ref[rows, cols] = dk
            dv_ref[rows, cols] = dv
            if c > 0:
                state = state + nn(qt_ref[cols, rows], mg)


def finish_kernel(per, me_ref, k_ref, v_ref, dki_ref, dvi_ref, e0, e1, e2, e3, dk_ref, dv_ref):
    tokens = k_ref.shape[0]
    me = me_ref[0]
    for s, e_ref in enumerate((e0, e1, e2, e3)):
        for j in range(per):
            cols = head_cols(me ^ s, j, per)
            suffix = e_ref[pl.ds(j * D, D), :].astype(BF16)
            for c in range(tokens // CHUNK):
                rows = pl.ds(c * CHUNK, CHUNK)
                dk_ref[rows, cols] = (dki_ref[rows, cols] + nt(v_ref[rows, cols], suffix)).astype(BF16)
                dv_ref[rows, cols] = (dvi_ref[rows, cols] + nn(k_ref[rows, cols], suffix)).astype(BF16)


def swap(x, n, mask):
    return lax.ppermute(x, "ctx", [(i, i ^ mask) for i in range(n)])


def scan_states(slots, me, n, ahead):
    low = me & (GROUP - 1)
    got = [slots[0]] + [swap(slots[s], n, s) for s in range(1, GROUP)]

    def before(a, b):
        return (a < b) if ahead else (a > b)

    total = (got[0] + got[1]) + (got[2] + got[3])
    carry = None
    step = GROUP
    while step < n:
        other = swap(total, n, step)
        kept = jnp.where(before(me ^ step, me), other, 0.0)
        carry = kept if carry is None else carry + kept
        step *= 2
        if step < n:
            total = total + other
    sums = []
    for s in range(GROUP):
        mine = low ^ s
        part = carry
        for t in range(GROUP):
            if t != s:
                term = jnp.where(before(low ^ t, mine), got[t], 0.0)
                part = term if part is None else part + term
        sums.append(part)
    return [sums[0]] + [swap(sums[s], n, s) for s in range(1, GROUP)]


def shards(n, q, k, v, norm_gain, dy):
    tokens, width = q.shape
    heads = width // D
    per = heads // GROUP
    full_width = HEADS * D
    me = lax.axis_index("ctx").astype(jnp.int32)
    low = (me & (GROUP - 1)).reshape(1)
    gain = norm_gain.reshape(1, width)
    state = jax.ShapeDtypeStruct((per * D, D), F32)
    wide = jax.ShapeDtypeStruct((tokens, width), F32)
    narrow = jax.ShapeDtypeStruct((tokens, width), BF16)
    unit = 2 * tokens * D * D

    def states(slots):
        kernel = functools.partial(state_kernel, slots, per)
        return call(kernel, "state", [state] * len(slots), [low, k, v], unit * per * len(slots))

    s1, s2, s3 = states((1, 2, 3))
    (s0,) = states((0,))
    intra, qt = call(intra_kernel, "intra", [wide, jax.ShapeDtypeStruct((width, tokens), BF16)], [q, k, v], 6 * unit * heads)
    pre = scan_states([s0, s1, s2, s3], me, n, True)

    acc = pltpu.VMEM((tokens, D), F32)
    mixed, red = call(
        functools.partial(mix_kernel, per), "mix", [wide, jax.ShapeDtypeStruct((2, tokens), F32)],
        [low, q, intra, dy, gain] + pre, unit * heads, scratch=(acc, acc))
    red = lax.psum(red, "fsdp")

    mg, g1, g2, g3, g0 = call(
        functools.partial(grad_kernel, (1, 2, 3, 0), per, full_width), "grad", [narrow] + [state] * 4,
        [low, qt, mixed, dy, gain, red], unit * heads)
    dki, dvi = call(keyvalue_kernel, "keyvalue", [wide, wide], [q, k, v, qt, mg], 11 * unit * heads)
    att, dq = call(
        functools.partial(query_kernel, per, full_width), "query", [narrow, narrow],
        [low, k, v, mg, mixed, gain, red] + pre, 6 * unit * heads)
    suf = scan_states([g0, g1, g2, g3], me, n, False)
    dk, dv = call(
        functools.partial(finish_kernel, per), "finish", [narrow, narrow],
        [low, k, v, dki, dvi] + suf, 2 * unit * heads)
    return att, dq, dk, dv


def solution(mesh):
    in_specs = (P("ctx", "fsdp"), P("ctx", "fsdp"), P("ctx", "fsdp"), P("fsdp"), P("ctx", "fsdp"))
    out_specs = (P("ctx", "fsdp"),) * 4
    body = functools.partial(shards, mesh.shape["ctx"])
    return jax.shard_map(body, mesh=mesh, in_specs=in_specs, out_specs=out_specs, check_vma=False)
```

```python
import functools

import jax
import jax.numpy as jnp
from jax import lax
from jax.experimental import pallas as pl
from jax.experimental.pallas import tpu as pltpu
from jax.sharding import PartitionSpec as P


HEADS = 32
HEAD_DIM = 128
GROUP = 4
CHUNK = 256
ROWS = 128

F32 = jnp.float32
BF16 = jnp.bfloat16
D = HEAD_DIM


def nn(a, b):
    return lax.dot_general(a, b, (((1,), (0,)), ((), ())), preferred_element_type=F32)


def nt(a, b):
    return lax.dot_general(a, b, (((1,), (1,)), ((), ())), preferred_element_type=F32)


def tn(a, b):
    return lax.dot_general(a, b, (((0,), (0,)), ((), ())), preferred_element_type=F32)


def slot_cols(me, s, wide):
    return pl.ds(pl.multiple_of((me ^ s) * wide, D), wide)


def head_cols(me, s, j, wide):
    return pl.ds(pl.multiple_of((me ^ s) * wide + j * D, D), D)


def diagonal(blocks):
    if len(blocks) == 1:
        return blocks[0]
    zero = jnp.zeros_like(blocks[0])
    lines = [jnp.concatenate([b if i == j else zero for j in range(len(blocks))], 1) for i, b in enumerate(blocks)]
    return jnp.concatenate(lines, 0)


def heads_of(ref, per):
    return [ref[pl.ds(j * D, D), :] for j in range(per)]


VMEM, HBM, SMEM = pltpu.VMEM, pltpu.HBM, pltpu.SMEM


def call(kernel, outs, args, flops, out_spaces=None, in_spaces=None, scratch=(), vmem=4):
    in_spaces = in_spaces or [SMEM if x.dtype == jnp.int32 else VMEM for x in args]
    out_spaces = out_spaces or [VMEM for _ in outs]
    size = sum(x.size * x.dtype.itemsize for x in args)
    return pl.pallas_call(
        kernel,
        out_shape=outs,
        in_specs=[pl.BlockSpec(memory_space=s) for s in in_spaces],
        out_specs=[pl.BlockSpec(memory_space=s) for s in out_spaces],
        scratch_shapes=list(scratch),
        cost_estimate=pl.CostEstimate(flops=flops, bytes_accessed=size, transcendentals=0),
        compiler_params=pltpu.CompilerParams(vmem_limit_bytes=vmem << 20),
    )(*args)


def state_kernel(per, me_ref, k_hbm, v_hbm, k_ref, v_ref, s1, s2, s3, sems):
    me = me_ref[0] & (GROUP - 1)
    copies = []
    for i, s in enumerate((1, 2, 3, 0)):
        cols = slot_cols(me, s, per * D)
        pair = [
            pltpu.make_async_copy(src.at[:, cols], dst.at[:, cols], sems.at[2 * i + n])
            for n, (src, dst) in enumerate(((k_hbm, k_ref), (v_hbm, v_ref)))
        ]
        for copy in pair:
            copy.start()
        copies.append(pair)
    for pair, s, out_ref in zip(copies, (1, 2, 3), (s1, s2, s3)):
        for copy in pair:
            copy.wait()
        for j in range(per):
            cols = head_cols(me, s, j, per * D)
            out_ref[pl.ds(j * D, D), :] = tn(k_ref[:, cols], v_ref[:, cols])
    for copy in copies[3]:
        copy.wait()


def own_kernel(per, me_ref, k_ref, v_ref, q_hbm, dy_hbm, s0, q_ref, dy_ref, sems):
    me = me_ref[0] & (GROUP - 1)
    copies = [
        pltpu.make_async_copy(q_hbm, q_ref, sems.at[0]),
        pltpu.make_async_copy(dy_hbm, dy_ref, sems.at[1]),
    ]
    for copy in copies:
        copy.start()
    for j in range(per):
        cols = head_cols(me, 0, j, per * D)
        s0[pl.ds(j * D, D), :] = tn(k_ref[:, cols], v_ref[:, cols])
    for copy in copies:
        copy.wait()


def lower_mask(transposed):
    row = lax.broadcasted_iota(jnp.int32, (CHUNK, CHUNK), 0)
    col = lax.broadcasted_iota(jnp.int32, (CHUNK, CHUNK), 1)
    return (row <= col) if transposed else (row >= col)


def intra_kernel(slots, per, me_ref, q_ref, k_ref, v_ref, mixed_ref, qt_ref, pt_ref, st_ref):
    tokens = q_ref.shape[0]
    me = me_ref[0] & (GROUP - 1)
    causal, upper = lower_mask(False), lower_mask(True)
    for i, s in enumerate(slots):
        for j in range(per):
            cols = head_cols(me, s, j, per * D)
            own = pl.ds((i * per + j) * D, D)
            state = jnp.zeros((D, D), F32)
            for c in range(tokens // CHUNK):
                rows = pl.ds(c * CHUNK, CHUNK)
                q, k, v = q_ref[rows, cols], k_ref[rows, cols], v_ref[rows, cols]
                probs = jnp.where(causal, nt(q, k), 0.0).astype(BF16)
                out = nn(probs, v)
                if c > 0:
                    out = out + nn(q, state.astype(BF16))
                mixed_ref[rows, own] = out
                pt_ref[i * per + j, rows, :] = jnp.where(upper, nt(k, q), 0.0).astype(BF16)
                qt_ref[own, rows] = q.T
                st_ref[i * per + j, pl.ds(c * D, D), :] = state
                if (c + 1) * CHUNK < tokens:
                    state = state + tn(k, v)


def mix_kernel(per, halves, me_ref, q_ref, dy_ref, gain_ref, e0, e1, e2, e3, in0, in1, mixed_ref, red_ref, sq, cr):
    tokens = q_ref.shape[0]
    me = me_ref[0] & (GROUP - 1)
    wide = per * D
    for s, e_ref in enumerate((e0, e1, e2, e3)):
        cols = slot_cols(me, s, wide)
        intra_ref = (in0, in1)[s // halves]
        own = pl.ds((s % halves) * wide, wide)
        prefix = diagonal([e.astype(BF16) for e in heads_of(e_ref, per)])
        gain = gain_ref[:, cols].astype(F32)
        for c in range(tokens // ROWS):
            rows = pl.ds(c * ROWS, ROWS)
            mixed = intra_ref[rows, own] + nn(q_ref[rows, cols], prefix)
            mixed_ref[rows, cols] = mixed
            weighted = dy_ref[rows, cols].astype(F32) * gain * mixed
            square = mixed * mixed
            square = sum(square[:, j * D:(j + 1) * D] for j in range(per))
            weighted = sum(weighted[:, j * D:(j + 1) * D] for j in range(per))
            if s == 0:
                sq[rows, :] = square
                cr[rows, :] = weighted
            else:
                sq[rows, :] += square
                cr[rows, :] += weighted
    ones = jnp.ones((8, D), F32)
    dims = (((1,), (1,)), ((), ()))
    for i, acc in enumerate((sq, cr)):
        total = lax.dot_general(ones, acc[...], dims, precision=lax.Precision.HIGHEST, preferred_element_type=F32)
        red_ref[pl.ds(i, 1), :] = total[:1]


def row_scales(red_ref, full_width):
    inverse = lax.rsqrt(red_ref[0:1, :] / full_width + 1e-06)
    factor = inverse * inverse * red_ref[1:2, :] / full_width
    return inverse, factor


def spread(row, c):
    return jnp.broadcast_to(row[:, c * ROWS:(c + 1) * ROWS], (D, ROWS)).T


def grad_kernel(per, halves, full_width, me_ref, qt0, qt1, mixed_ref, dy_ref, gain_ref, red_ref, mg_ref, g0, g1, g2, g3):
    tokens, width = mixed_ref.shape
    me = me_ref[0] & (GROUP - 1)
    inverse, factor = row_scales(red_ref, full_width)
    for c in range(tokens // ROWS):
        rows = pl.ds(c * ROWS, ROWS)
        inv, fac = spread(inverse, c), spread(factor, c)
        for h in range(width // D):
            cols = pl.ds(h * D, D)
            weighted = dy_ref[rows, cols].astype(F32) * gain_ref[:, cols].astype(F32)
            mg_ref[rows, cols] = (inv * (weighted - mixed_ref[rows, cols] * fac)).astype(BF16)
    for s in (1, 2, 3, 0):
        out_ref = (g0, g1, g2, g3)[s]
        for j in range(per):
            own = pl.ds(((s % halves) * per + j) * D, D)
            cols = head_cols(me, s, j, per * D)
            out_ref[pl.ds(j * D, D), :] = nn((qt0, qt1)[s // halves][own, :], mg_ref[:, cols])


def query_kernel(per, halves, full_width, me_ref, k_ref, v_ref, mg_ref, mixed_ref, gain_ref, red_ref, e0, e1, e2, e3, st0, st1, att_hbm, dq_hbm, att, dq, sems):
    tokens, width = k_ref.shape
    me = me_ref[0] & (GROUP - 1)
    wide = per * D
    causal = lower_mask(False)
    inverse, _ = row_scales(red_ref, full_width)
    for c in range(tokens // ROWS):
        rows = pl.ds(c * ROWS, ROWS)
        inv = spread(inverse, c)
        for h in range(width // D):
            cols = pl.ds(h * D, D)
            att[rows, cols] = (mixed_ref[rows, cols] * inv * gain_ref[:, cols].astype(F32)).astype(BF16)
    copies = [pltpu.make_async_copy(att, att_hbm, sems.at[GROUP])]
    copies[0].start()
    for s, e_ref in enumerate((e0, e1, e2, e3)):
        cols = slot_cols(me, s, wide)
        st_ref = (st0, st1)[s // halves]
        prefix = heads_of(e_ref, per)
        for c in range(tokens // CHUNK):
            rows = pl.ds(c * CHUNK, CHUNK)
            states = [prefix[j] + st_ref[(s % halves) * per + j, pl.ds(c * D, D), :] if c else prefix[j] for j in range(per)]
            far = nt(mg_ref[rows, cols], diagonal([x.astype(BF16) for x in states]))
            for j in range(per):
                one = head_cols(me, s, j, wide)
                ds = jnp.where(causal, nt(mg_ref[rows, one], v_ref[rows, one]), 0.0).astype(BF16)
                dq[rows, one] = (nn(ds, k_ref[rows, one]) + far[:, j * D:(j + 1) * D]).astype(BF16)
        copies.append(pltpu.make_async_copy(dq.at[:, cols], dq_hbm.at[:, cols], sems.at[s]))
        copies[-1].start()
    for copy in copies:
        copy.wait()


def keyvalue_kernel(slots, per, me_ref, q_ref, k_ref, v_ref, mg_ref, qt_ref, pt_ref, dk_ref, dv_ref):
    tokens = q_ref.shape[0]
    me = me_ref[0] & (GROUP - 1)
    wide = per * D
    upper = lower_mask(True)
    for i, s in enumerate(slots):
        pair = slot_cols(me, s, wide)
        states = [jnp.zeros((D, D), F32) for _ in range(per)]
        for c in reversed(range(tokens // CHUNK)):
            rows = pl.ds(c * CHUNK, CHUNK)
            last = (c + 1) * CHUNK == tokens
            if not last:
                later = diagonal([x.astype(BF16) for x in states])
                far_k = nt(v_ref[rows, pair], later)
                far_v = nn(k_ref[rows, pair], later)
            for j in range(per):
                own = pl.ds((i * per + j) * D, D)
                cols = head_cols(me, s, j, wide)
                mg = mg_ref[rows, cols]
                ds = jnp.where(upper, nt(v_ref[rows, cols], mg), 0.0).astype(BF16)
                dk = nn(ds, q_ref[rows, cols])
                dv = nn(pt_ref[i * per + j, rows, :], mg)
                if not last:
                    dk = dk + far_k[:, j * D:(j + 1) * D]
                    dv = dv + far_v[:, j * D:(j + 1) * D]
                dk_ref[rows, own] = dk
                dv_ref[rows, own] = dv
                if c > 0:
                    states[j] = states[j] + nn(qt_ref[own, rows], mg)


def finish_kernel(per, halves, me_ref, k_ref, v_ref, e0, e1, e2, e3, dk0, dk1, dv0, dv1, dk_hbm, dv_hbm, dk, dv, sems):
    tokens = k_ref.shape[0]
    me = me_ref[0] & (GROUP - 1)
    wide = per * D
    copies = []
    for s, e_ref in enumerate((e0, e1, e2, e3)):
        cols = slot_cols(me, s, wide)
        own = pl.ds((s % halves) * wide, wide)
        suffix = diagonal([e.astype(BF16) for e in heads_of(e_ref, per)])
        for c in range(tokens // ROWS):
            rows = pl.ds(c * ROWS, ROWS)
            dk[rows, cols] = ((dk0, dk1)[s // halves][rows, own] + nt(v_ref[rows, cols], suffix)).astype(BF16)
            dv[rows, cols] = ((dv0, dv1)[s // halves][rows, own] + nn(k_ref[rows, cols], suffix)).astype(BF16)
        for n, (src, dst) in enumerate(((dk, dk_hbm), (dv, dv_hbm))):
            copies.append(pltpu.make_async_copy(src.at[:, cols], dst.at[:, cols], sems.at[2 * s + n]))
            copies[-1].start()
    for copy in copies:
        copy.wait()


def swap(x, axis, n, mask):
    return lax.ppermute(x, axis, [(i, i ^ mask) for i in range(n)])


def total_kernel(*refs):
    *in_refs, out_ref = refs
    out_ref[...] = functools.reduce(lambda x, y: x + y, [r[...] for r in in_refs])


def before(a, b, ahead):
    return (a < b) if ahead else (a > b)


def masked(flag, x):
    return jnp.where(flag, x, 0.0)


def sums_kernel(ahead, steps, me_ref, *refs):
    me = me_ref[0]
    low = me & (GROUP - 1)
    got, others, outs = refs[:GROUP], refs[GROUP:GROUP + len(steps)], refs[GROUP + len(steps):]
    for j in range(outs[0].shape[0] // D):
        rows = pl.ds(j * D, D)
        carry = jnp.zeros((D, D), F32)
        for step, other in zip(steps, others):
            carry = carry + masked(before(me ^ step, me, ahead), other[rows, :])
        parts = [r[rows, :] for r in got]
        for s in range(GROUP):
            outs[s][rows, :] = carry + sum(
                masked(before(low ^ t, low ^ s, ahead), parts[t]) for t in range(GROUP) if t != s)


def scan_states(slots, me, n, ahead):
    got = [slots[0]] + [swap(slots[s], "ctx", n, s) for s in range(1, GROUP)]
    like = jax.ShapeDtypeStruct(slots[0].shape, F32)
    steps, others = [], []
    step = GROUP
    while step < n:
        (total,) = call(total_kernel, [like], got if step == GROUP else [total, others[-1]], 0)
        others.append(swap(total, "ctx", n, step))
        steps.append(step)
        step *= 2
    sums = call(
        functools.partial(sums_kernel, ahead, tuple(steps)), [like] * GROUP,
        [me, *got, *others], 0)
    return [sums[0]] + [swap(sums[s], "ctx", n, s) for s in range(1, GROUP)]


def shards(n, m, q, k, v, norm_gain, dy):
    return program(n, m, q, k, v, norm_gain, dy)


def program(n, m, q, k, v, norm_gain, dy):
    tokens, width = q.shape
    heads = width // D
    per = heads // GROUP
    halves = GROUP // 2
    half = width // 2
    full_width = HEADS * D
    me = lax.axis_index("ctx").astype(jnp.int32).reshape(1)
    gain = norm_gain.reshape(1, width)

    def shape(dtype, *dims):
        return jax.ShapeDtypeStruct(dims, dtype)

    state = shape(F32, per * D, D)
    wide = shape(F32, tokens, width)
    narrow = shape(BF16, tokens, width)
    unit = 2 * tokens * D * D
    part = functools.partial
    pairs = ((0, 1), (2, 3))

    q, k, v, dy = [pltpu.with_memory_space_constraint(x, pltpu.HBM) for x in (q, k, v, dy)]
    k, v, s1, s2, s3 = call(
        part(state_kernel, per), [narrow, narrow, state, state, state], [me, k, v],
        unit * heads, in_spaces=[SMEM, HBM, HBM], scratch=[pltpu.SemaphoreType.DMA((8,))])
    s0, q, dy = call(
        part(own_kernel, per), [state, narrow, narrow], [me, k, v, q, dy],
        unit * per, in_spaces=[SMEM, VMEM, VMEM, HBM, HBM], scratch=[pltpu.SemaphoreType.DMA((2,))])
    kept = [
        shape(F32, tokens, half), shape(BF16, half, tokens),
        shape(BF16, heads // 2, tokens, CHUNK), shape(F32, heads // 2, tokens // CHUNK * D, D)]
    fronts = [
        call(part(intra_kernel, pairs[i], per), kept, [me, q, k, v], 4 * unit * heads)
        for i in range(2)]
    intra, qt, pt, st = zip(*fronts)
    pre = scan_states([s0, s1, s2, s3], me, n, True)

    acc = pltpu.VMEM((tokens, D), F32)
    mixed, red = call(
        part(mix_kernel, per, halves), [wide, shape(F32, 2, tokens)],
        [me, q, dy, gain, *pre, *intra], unit * heads, scratch=(acc, acc))
    mask = 1
    while mask < m:
        red = red + swap(red, "fsdp", m, mask)
        mask *= 2

    mg, g0, g1, g2, g3 = call(
        part(grad_kernel, per, halves, full_width), [narrow] + [state] * 4,
        [me, *qt, mixed, dy, gain, red], unit * heads)
    whole = pltpu.VMEM((tokens, width), BF16)
    att, dq = call(
        part(query_kernel, per, halves, full_width), [narrow, narrow],
        [me, k, v, mg, mixed, gain, red, *pre, *st], 6 * unit * heads,
        out_spaces=[HBM, HBM], scratch=[whole, whole, pltpu.SemaphoreType.DMA((GROUP + 1,))], vmem=6)
    backs = [
        call(part(keyvalue_kernel, pairs[i], per), [shape(F32, tokens, half)] * 2,
             [me, q, k, v, mg, qt[i], pt[i]], 4 * unit * heads)
        for i in range(2)]
    dki, dvi = zip(*backs)
    suf = scan_states([g0, g1, g2, g3], me, n, False)
    dk, dv = call(
        part(finish_kernel, per, halves), [narrow, narrow],
        [me, k, v, *suf, *dki, *dvi], 2 * unit * heads,
        out_spaces=[HBM, HBM], scratch=[whole, whole, pltpu.SemaphoreType.DMA((2 * GROUP,))], vmem=6)
    return att, dq, dk, dv


def solution(mesh):
    in_specs = (P("ctx", "fsdp"), P("ctx", "fsdp"), P("ctx", "fsdp"), P("fsdp"), P("ctx", "fsdp"))
    out_specs = (P("ctx", "fsdp"),) * 4
    body = functools.partial(shards, mesh.shape["ctx"], mesh.shape["fsdp"])
    return jax.shard_map(body, mesh=mesh, in_specs=in_specs, out_specs=out_specs, check_vma=False)
```
